32 devices in a mesh: seq: 8 (over z, y), head: 4 (over x, core).
Axes of the slice: x: 2, y: 2, z: 4, core: 2. Of those that a mesh axis runs over, the one named last changes fastest.
Arguments:
- tokens: bfloat16 [8192, 2048], P('seq'), may hold values from -6 to 6
- w_query: bfloat16 [2048, 2048], P(None, 'head'), may hold values from -0.125 to 0.125
- w_key: bfloat16 [2048, 2048], P(None, 'head'), may hold values from -0.125 to 0.125
- w_value: bfloat16 [2048, 2048], P(None, 'head'), may hold values from -0.125 to 0.125
- w_out: bfloat16 [2048, 2048], P('head'), may hold values from -0.125 to 0.125
- norm_gain: float32 [2048], P('head'), may hold values from 0.5 to 1.5
- forget_rate: float32 [8192, 16], P('seq', 'head'), may hold values from 0 to 2, as said below
- routing: int32 [128, 16, 2], P('seq', 'head'), may hold values from 0 to 7, all different within a row
- memory_blend_share: float32 [128, 16, 2], P('seq', 'head'), may hold values from 0.25 to 1
Outputs:
- mixed: bfloat16 [8192, 2048], P(('seq', 'head'))
The draws below stay inside these ranges and needn't reach their ends.
Inputs may be any that keep to these rules, and one draw needn't show every extreme that they name: `routing`: each block and head names 2 different memories. `forget_rate`: positive rates.
All inputs are finite; a program needn't handle non-finite values.
Results may differ from the reference program's by a relative error of at most 0.03.
Values may be sent and summed in bfloat16 or wider, within the bound.
A program may use at most 128 MiB of HBM per device.

```python
import math
import jax
import jax.numpy as jnp
from jax import lax

D = 2048
ATTENTION_GROUPS = 16
HD = 128
M = 8
TOP = 2
CH = 64
TOKENS = 8192
BLOCKS = 128


def draw_forget_rate(key, part):
    quick_seed_state = jax.random.fold_in(key, 11)
    key_jitter = jax.random.fold_in(key, 12)
    key_spots = jax.random.fold_in(key, 13)
    spell_seed_state = jax.random.fold_in(key, 14)
    writes = TOKENS * TOP / M
    fast_share = 5
    is_fast = jax.random.randint(quick_seed_state, (ATTENTION_GROUPS,), 0, 10) < fast_share
    base = jnp.where(is_fast, 0.025, 0.25 / writes)
    jitter = jnp.exp(jax.random.uniform(key_jitter, (TOKENS, ATTENTION_GROUPS), jnp.float32, -math.log(2.0), math.log(2.0)))
    retention_fades = base[None, :] * jitter
    spots = jax.random.randint(key_spots, (3, ATTENTION_GROUPS), 0, TOKENS)
    spell_durations = jax.random.uniform(spell_seed_state, (3, ATTENTION_GROUPS), jnp.float32, 0.22, 0.45)
    memory_selection_tally = jnp.arange(TOKENS)[:, None, None] == spots[None, :, :]
    retention_fades = retention_fades + jnp.sum(jnp.where(memory_selection_tally, spell_durations[None, :, :], 0.0), axis=1)
    return retention_fades.astype(jnp.float32)


def block_levels(rng, shape, pieces, least, top_value):
    level, own = 1.0, jax.random.fold_in(rng, 6)
    for position, parts in pieces:
        heights = jnp.exp(jax.random.uniform(jax.random.fold_in(own, position), (parts,), jnp.float32, least / len(pieces), top_value / len(pieces)))
        level = level * jnp.repeat(heights, shape[position] // parts).reshape([-1 if axis == position else 1 for axis in range(len(shape))])
    return level


def choose_distinct(stream_key, rows, count, top, lift):
    sequence = jax.random.permutation(jax.random.fold_in(stream_key, 1), count)
    pull = sequence
    for power in range(3):
        pull = pull * pull // count
    pull = pull * lift // count
    tickets = jax.random.randint(jax.random.fold_in(stream_key, 2), (rows, count), 0, 4096) + pull
    fixed_rows = jax.random.permutation(jax.random.fold_in(stream_key, 3), rows)[jnp.arange(count) % rows]
    tickets = jnp.where(jnp.arange(rows)[:, None] == fixed_rows[None, :], 1 << 14, tickets)
    score = tickets * count + jnp.arange(count)
    return lax.top_k(score.astype(jnp.int32), top)[1].astype(jnp.int32)


def scatter_about(key, dims, spread, bound, pieces=(), held_as=jnp.bfloat16):
    values = spread * jax.random.normal(key, dims, jnp.float32)
    if pieces:
        values = values * block_levels(key, dims, pieces, -0.22, 0.18)
    return jnp.clip(values, -bound, bound).astype(held_as)


def setup_inputs(seed: int = 0) -> dict:
    splits = jax.random.split(jax.random.key(seed), 10)
    tokens = scatter_about(splits[0], (TOKENS, D), 1.0, 6.0, ((0, 8),))
    w_query = scatter_about(splits[1], (D, ATTENTION_GROUPS * HD), D ** -0.5, 0.125, ((1, 4),))
    w_key = scatter_about(splits[2], (D, ATTENTION_GROUPS * HD), D ** -0.5, 0.125, ((1, 4),))
    w_value = scatter_about(splits[3], (D, ATTENTION_GROUPS * HD), D ** -0.5, 0.125, ((1, 4),))
    w_out = scatter_about(splits[4], (ATTENTION_GROUPS * HD, D), (ATTENTION_GROUPS * HD) ** -0.5, 0.125, ((0, 4),))
    norm_gain = jnp.clip(1.0 + 0.1 * jax.random.normal(splits[5], (ATTENTION_GROUPS * HD,), jnp.float32), 0.5, 1.5)
    forget_rate = draw_forget_rate(jax.random.fold_in(splits[9], 71), 0)
    routing = choose_distinct(splits[7], BLOCKS * ATTENTION_GROUPS, M, TOP, 2048).reshape((BLOCKS, ATTENTION_GROUPS, TOP))
    memory_blend_share = jnp.clip(0.25 + 0.75 * jax.random.uniform(splits[8], (BLOCKS, ATTENTION_GROUPS, TOP), jnp.float32) ** block_levels(splits[8], (BLOCKS, ATTENTION_GROUPS, TOP), ((0, 8), (1, 4)), -0.2, 0.2), 0.25, 1.0)
    return {"tokens": tokens, "w_query": w_query, "w_key": w_key, "w_value": w_value, "w_out": w_out, "norm_gain": norm_gain, "forget_rate": forget_rate, "routing": routing, "memory_blend_share": memory_blend_share}


HIGH = lax.Precision.HIGHEST

def block_step(memory, inputs):
    query, key_raw, value_raw, retention_fades, chosen, weights = inputs
    heads_all = retention_fades.shape[1]
    query = query.astype(jnp.float32).reshape(CH, heads_all, HD).transpose(1, 0, 2)
    key_rows = key_raw.astype(jnp.float32).reshape(CH, heads_all, HD).transpose(1, 0, 2)
    key_rows = key_rows * lax.rsqrt(lax.optimization_barrier(jnp.sum(key_rows * key_rows, axis=-1, keepdims=True)) + 1e-06)
    key_rows = key_rows.astype(jnp.bfloat16).astype(jnp.float32)
    value_rows = value_raw.astype(jnp.float32).reshape(CH, heads_all, HD).transpose(1, 0, 2)
    cumul = jnp.cumsum(-retention_fades.transpose(1, 0), axis=1)
    block_end = cumul[:, -1]
    positions = jnp.arange(CH)
    causal = positions[:, None] >= positions[None, :]
    gaps = cumul[:, :, None] - cumul[:, None, :]
    decays = jnp.where(causal, jnp.exp(jnp.where(causal, gaps, 0.0)), 0.0)
    scores = jnp.einsum('hqd,hkd->hqk', query, key_rows, precision=HIGH)
    weighted = (scores * decays).astype(jnp.bfloat16).astype(jnp.float32)
    within = jnp.einsum('hqk,hkd->hqd', weighted, value_rows, precision=HIGH)
    one_hot = (chosen[:, :, None] == jnp.arange(M)[None, None, :]).astype(jnp.float32)
    routed = lax.optimization_barrier(jnp.sum(one_hot, axis=1))
    mix_weight = lax.optimization_barrier(jnp.sum(weights[:, :, None] * one_hot, axis=1))
    mixed_state = jnp.einsum('hm,hmde->hde', mix_weight, memory, precision=HIGH)
    carried_part = jnp.exp(cumul)[:, :, None] * jnp.einsum('hqd,hde->hqe', query, mixed_state, precision=HIGH)
    attended_output = carried_part + lax.optimization_barrier(jnp.sum(weights, axis=1))[:, None, None] * within
    scaled_keys = key_rows * jnp.exp(block_end[:, None] - cumul)[:, :, None]
    scaled_keys = scaled_keys.astype(jnp.bfloat16).astype(jnp.float32)
    written = jnp.einsum('hsd,hse->hde', scaled_keys, value_rows, precision=HIGH)
    factor = jnp.where(routed > 0, jnp.exp(block_end)[:, None], 1.0)
    memory = memory * factor[:, :, None, None] + routed[:, :, None, None] * written[:, None]
    return (memory, attended_output.transpose(1, 0, 2))

def reference(tokens, w_query, w_key, w_value, w_out, norm_gain, forget_rate, routing, memory_blend_share):
    query = jnp.dot(tokens, w_query, preferred_element_type=jnp.float32).astype(jnp.bfloat16)
    key_raw = jnp.dot(tokens, w_key, preferred_element_type=jnp.float32).astype(jnp.bfloat16)
    value_raw = jnp.dot(tokens, w_value, preferred_element_type=jnp.float32).astype(jnp.bfloat16)
    num_blocks = TOKENS // CH
    inputs = (query.reshape(num_blocks, CH, ATTENTION_GROUPS * HD), key_raw.reshape(num_blocks, CH, ATTENTION_GROUPS * HD), value_raw.reshape(num_blocks, CH, ATTENTION_GROUPS * HD), forget_rate.reshape(num_blocks, CH, ATTENTION_GROUPS), routing, memory_blend_share)
    memory = jnp.zeros((ATTENTION_GROUPS, M, HD, HD), jnp.float32)
    memory, attended_output = lax.scan(block_step, memory, inputs)
    attended_output = attended_output.reshape(TOKENS, ATTENTION_GROUPS, HD)
    normed = attended_output * lax.rsqrt(lax.optimization_barrier(jnp.mean(attended_output * attended_output, axis=-1, keepdims=True)) + 1e-06)
    normed = (normed * norm_gain.reshape(ATTENTION_GROUPS, HD)).astype(jnp.bfloat16).reshape(TOKENS, ATTENTION_GROUPS * HD)
    return jnp.dot(normed, w_out, preferred_element_type=jnp.float32).astype(jnp.bfloat16)
```

```python
import functools

import jax
import jax.numpy as jnp
from jax import lax
from jax.experimental import pallas as pl
from jax.experimental.pallas import tpu as pltpu
from jax.sharding import PartitionSpec as P

HD = 128
M = 8
CH = 64

HIGH = lax.Precision.HIGHEST
MESH = pl.DeviceIdType.MESH
VMEM = pltpu.VMEM
SMEM = pltpu.SMEM
LIMIT = 60 * 1024 * 1024


def local_kernel(
    chosen, shares, fades, q_ref, k_ref, v_ref, column_ref, row_ref, att_ref, mem_ref
):
    blocks, local_heads = row_ref.shape[0], row_ref.shape[1]
    mem_ref[...] = jnp.zeros_like(mem_ref)
    t = lax.broadcasted_iota(jnp.int32, (CH, CH), 0)
    s = lax.broadcasted_iota(jnp.int32, (CH, CH), 1)
    causal = t >= s

    def block(b, carry):
        rows = pl.ds(pl.multiple_of(b * CH, CH), CH)
        for h in range(local_heads):
            cols = slice(h * HD, (h + 1) * HD)
            query = q_ref[rows, cols]
            wide = k_ref[rows, cols].astype(jnp.float32)
            values = v_ref[rows, cols]
            keys = wide * lax.rsqrt(jnp.sum(wide * wide, axis=-1, keepdims=True) + 1e-06)
            keys = keys.astype(jnp.bfloat16)
            column = column_ref[rows, h : h + 1]
            line = row_ref[b, h : h + 1, :]
            gaps = jnp.where(causal, column - line, 0.0)
            decays = jnp.where(causal, jnp.exp(gaps), 0.0)
            scores = lax.dot_general(
                query, keys, (((1,), (1,)), ((), ())), preferred_element_type=jnp.float32
            )
            weighted = (scores * decays).astype(jnp.bfloat16)
            within = jnp.dot(weighted, values, preferred_element_type=jnp.float32)
            ending = column[CH - 1 : CH]
            scaled = (keys.astype(jnp.float32) * jnp.exp(ending - column)).astype(jnp.bfloat16)
            written = lax.dot_general(
                scaled, values, (((0,), (0,)), ((), ())), preferred_element_type=jnp.float32
            )
            at = (b * local_heads + h) * 2
            first, second = chosen[at], chosen[at + 1]
            share_a, share_b = shares[at], shares[at + 1]
            fade = fades[b * local_heads + h]
            old_a = mem_ref[h * M + first]
            old_b = mem_ref[h * M + second]
            mixed = (share_a * old_a + share_b * old_b).astype(jnp.bfloat16)
            carried = jnp.dot(query, mixed, preferred_element_type=jnp.float32)
            att_ref[rows, cols] = jnp.exp(column) * carried + (share_a + share_b) * within
            mem_ref[h * M + first] = fade * old_a + written
            mem_ref[h * M + second] = fade * old_b + written
        return carry

    lax.fori_loop(0, blocks, block, 0)


def chain_kernel(
    chosen,
    multipliers,
    products,
    mem_ref,
    q_ref,
    column_ref,
    att_ref,
    gain_ref,
    out_ref,
    inbox,
    outbox,
    current,
    send_sem,
    recv_sem,
):
    size, me = lax.axis_size("seq"), lax.axis_index("seq")
    pieces = mem_ref.shape[0]
    local_heads = pieces // M
    blocks = q_ref.shape[0] // CH
    barrier = pltpu.get_barrier_semaphore()

    @pl.when(me > 0)
    def _():
        pl.semaphore_signal(barrier, 1, device_id={"seq": me - 1}, device_id_type=MESH)

    @pl.when(me < size - 1)
    def _():
        pl.semaphore_signal(barrier, 1, device_id={"seq": me + 1}, device_id_type=MESH)

    peers = jnp.where(me > 0, 1, 0) + jnp.where(me < size - 1, 1, 0)
    pl.semaphore_wait(barrier, peers)

    @pl.when(me == 0)
    def _():
        inbox[...] = jnp.zeros_like(inbox)

    def copy(c):
        return pltpu.make_async_remote_copy(
            src_ref=outbox.at[c],
            dst_ref=inbox.at[c],
            send_sem=send_sem.at[c],
            recv_sem=recv_sem.at[c],
            device_id={"seq": me + 1},
            device_id_type=MESH,
        )

    for h in range(local_heads):

        def pass_on(m, carry):
            c = h * M + m

            @pl.when(me > 0)
            def _():
                copy(c).wait_recv()

            arrived = inbox[c].astype(jnp.float32)
            current[m] = arrived

            @pl.when(me < size - 1)
            def _():
                outbox[c] = (products[c] * arrived + mem_ref[c]).astype(jnp.bfloat16)
                copy(c).start()

            return carry

        lax.fori_loop(0, M, pass_on, 0)
        cols = slice(h * HD, (h + 1) * HD)

        def block(b, carry):
            rows = pl.ds(pl.multiple_of(b * CH, CH), CH)
            at = (b * local_heads + h) * 2
            entering = (
                multipliers[at] * current[chosen[at]]
                + multipliers[at + 1] * current[chosen[at + 1]]
            ).astype(jnp.bfloat16)
            carried = jnp.dot(q_ref[rows, cols], entering, preferred_element_type=jnp.float32)
            total = att_ref[rows, cols] + jnp.exp(column_ref[rows, h : h + 1]) * carried
            scale = lax.rsqrt(jnp.mean(total * total, axis=-1, keepdims=True) + 1e-06)
            out_ref[rows, cols] = (total * scale * gain_ref[:, cols]).astype(jnp.bfloat16)
            return carry

        lax.fori_loop(0, blocks, block, 0, unroll=4)

    @pl.when(me < size - 1)
    def _():
        def drain(c, carry):
            copy(c).wait_send()
            return carry

        lax.fori_loop(0, pieces, drain, 0)


def per_device(
    tokens, w_query, w_key, w_value, w_out, norm_gain, forget_rate, routing, memory_blend_share
):
    tok_rows = tokens.shape[0]
    local_heads = w_query.shape[1] // HD
    num_blocks = tok_rows // CH
    width = local_heads * HD
    whole_out = lax.all_gather(w_out, "head", axis=0, tiled=True)

    def project(weight):
        return jnp.dot(tokens, weight, preferred_element_type=jnp.float32).astype(jnp.bfloat16)

    key_raw, value_rows, query = project(w_key), project(w_value), project(w_query)
    cumul = jnp.cumsum(-forget_rate.reshape(num_blocks, CH, local_heads), axis=1)
    block_end = cumul[:, -1]
    column = cumul.reshape(tok_rows, local_heads)
    row = cumul.transpose(0, 2, 1)
    one_hot = (routing[..., None] == jnp.arange(M)).astype(jnp.float32)
    ends = jnp.sum(one_hot, axis=2) * block_end[:, :, None]
    before = jnp.arange(num_blocks)[:, None] > jnp.arange(num_blocks)[None, :]
    earlier = jnp.sum(jnp.where(before[:, :, None, None], ends[None], 0.0), axis=1)
    multipliers = memory_blend_share * jnp.sum(one_hot * jnp.exp(earlier)[:, :, None], axis=-1)
    products = jnp.exp(jnp.sum(ends, axis=0)).reshape(-1)
    chosen = routing.reshape(-1)

    smem = pl.BlockSpec(memory_space=SMEM)
    vmem = pl.BlockSpec(memory_space=VMEM)
    attended, memory = pl.pallas_call(
        local_kernel,
        out_shape=(
            jax.ShapeDtypeStruct((tok_rows, width), jnp.float32),
            jax.ShapeDtypeStruct((local_heads * M, HD, HD), jnp.float32),
        ),
        in_specs=[smem] * 3 + [vmem] * 5,
        out_specs=(vmem, vmem),
        compiler_params=pltpu.CompilerParams(vmem_limit_bytes=LIMIT),
        name="local",
    )(
        chosen,
        memory_blend_share.reshape(-1),
        jnp.exp(block_end).reshape(-1),
        query,
        key_raw,
        value_rows,
        column,
        row,
    )
    pieces = local_heads * M
    normed = pl.pallas_call(
        chain_kernel,
        out_shape=jax.ShapeDtypeStruct((tok_rows, width), jnp.bfloat16),
        in_specs=[smem] * 3 + [vmem] * 5,
        out_specs=vmem,
        scratch_shapes=[
            VMEM((pieces, HD, HD), jnp.bfloat16),
            VMEM((pieces, HD, HD), jnp.bfloat16),
            VMEM((M, HD, HD), jnp.float32),
            pltpu.SemaphoreType.DMA((pieces,)),
            pltpu.SemaphoreType.DMA((pieces,)),
        ],
        compiler_params=pltpu.CompilerParams(
            collective_id=0, has_side_effects=True, vmem_limit_bytes=LIMIT
        ),
        name="chain",
    )(chosen, multipliers.reshape(-1), products, memory, query, column, attended, norm_gain[None])
    exchanged = lax.all_to_all(normed, "head", split_axis=0, concat_axis=1, tiled=True)
    result = jnp.dot(exchanged, whole_out, preferred_element_type=jnp.float32)
    return result.astype(jnp.bfloat16)


def solution(mesh):
    placed = (
        P("seq", None),
        P(None, "head"),
        P(None, "head"),
        P(None, "head"),
        P("head", None),
        P("head"),
        P("seq", "head"),
        P("seq", "head", None),
        P("seq", "head", None),
    )
    return jax.shard_map(
        per_device, mesh=mesh, in_specs=placed, out_specs=P(("seq", "head"), None), check_vma=False
    )
```

```python
import jax
import jax.numpy as jnp
from jax import lax
from jax.experimental import pallas as pl
from jax.experimental.pallas import tpu as pltpu
from jax.sharding import PartitionSpec as P

HD = 128
M = 8
CH = 64

HIGH = lax.Precision.HIGHEST
MESH = pl.DeviceIdType.MESH
VMEM = pltpu.VMEM
SMEM = pltpu.SMEM
LIMIT = 60 * 1024 * 1024


def local_kernel(
    chosen, shares, q_ref, k_ref, v_ref, rate_ref, att_ref, mem_ref, growth_ref, entry_ref, prod_ref
):
    tok_rows, local_heads = rate_ref.shape
    blocks = tok_rows // CH
    mem_ref[...] = jnp.zeros_like(mem_ref)
    prod_ref[...] = jnp.ones_like(prod_ref)
    t = lax.broadcasted_iota(jnp.int32, (CH, CH), 0)
    s = lax.broadcasted_iota(jnp.int32, (CH, CH), 1)
    causal = t >= s

    def block(b, carry):
        rows = pl.ds(pl.multiple_of(b * CH, CH), CH)
        rates = rate_ref[rows, :]
        columns = -jnp.dot(
            jnp.where(t >= s, 1.0, 0.0), rates, precision=HIGH, preferred_element_type=jnp.float32
        )
        lines = -lax.dot_general(
            rates,
            jnp.where(t <= s, 1.0, 0.0),
            (((0,), (0,)), ((), ())),
            precision=HIGH,
            preferred_element_type=jnp.float32,
        )
        growths = jnp.exp(columns)
        growth_ref[rows, :] = growths
        for h in range(local_heads):
            cols = slice(h * HD, (h + 1) * HD)
            query = q_ref[rows, cols]
            wide = k_ref[rows, cols].astype(jnp.float32)
            values = v_ref[rows, cols]
            keys = wide * lax.rsqrt(jnp.sum(wide * wide, axis=-1, keepdims=True) + 1e-06)
            keys = keys.astype(jnp.bfloat16)
            column = columns[:, h : h + 1]
            line = lines[h : h + 1, :]
            gaps = jnp.where(causal, column - line, 0.0)
            decays = jnp.where(causal, jnp.exp(gaps), 0.0)
            scores = lax.dot_general(
                query, keys, (((1,), (1,)), ((), ())), preferred_element_type=jnp.float32
            )
            weighted = (scores * decays).astype(jnp.bfloat16)
            within = jnp.dot(weighted, values, preferred_element_type=jnp.float32)
            ending = column[CH - 1 : CH]
            scaled = (keys.astype(jnp.float32) * jnp.exp(ending - column)).astype(jnp.bfloat16)
            written = lax.dot_general(
                scaled, values, (((0,), (0,)), ((), ())), preferred_element_type=jnp.float32
            )
            at = (b * local_heads + h) * 2
            first, second = h * M + chosen[at], h * M + chosen[at + 1]
            share_a, share_b = shares[at], shares[at + 1]
            fade = jnp.broadcast_to(growths[CH - 1 : CH, h : h + 1], (1, HD))
            old_a = mem_ref[first]
            old_b = mem_ref[second]
            mixed = (share_a * old_a + share_b * old_b).astype(jnp.bfloat16)
            carried = jnp.dot(query, mixed, preferred_element_type=jnp.float32)
            att_ref[rows, cols] = (
                growths[:, h : h + 1] * carried + (share_a + share_b) * within
            )
            mem_ref[first] = fade * old_a + written
            mem_ref[second] = fade * old_b + written
            prod_a, prod_b = prod_ref[first], prod_ref[second]
            entry_ref[at] = share_a * prod_a
            entry_ref[at + 1] = share_b * prod_b
            prod_ref[first] = fade * prod_a
            prod_ref[second] = fade * prod_b
        return carry

    lax.fori_loop(0, blocks, block, 0)


def chain_kernel(
    chosen,
    entry_ref,
    prod_ref,
    mem_ref,
    q_ref,
    growth_ref,
    att_ref,
    gain_ref,
    w_hbm,
    out_ref,
    inbox,
    outbox,
    current,
    finished,
    exchanged,
    partial,
    w_ref,
    w_sem,
    send_sem,
    recv_sem,
    row_send,
    row_recv,
):
    size, me = lax.axis_size("seq"), lax.axis_index("seq")
    groups, mine = lax.axis_size("head"), lax.axis_index("head")
    pieces = mem_ref.shape[0]
    local_heads = pieces // M
    width = local_heads * HD
    blocks = q_ref.shape[0] // CH
    own_rows = q_ref.shape[0] // groups
    fetch = pltpu.make_async_copy(w_hbm, w_ref, w_sem)
    fetch.start()
    barrier = pltpu.get_barrier_semaphore()

    @pl.when(me > 0)
    def _():
        pl.semaphore_signal(barrier, 1, device_id={"seq": me - 1}, device_id_type=MESH)

    @pl.when(me < size - 1)
    def _():
        pl.semaphore_signal(barrier, 1, device_id={"seq": me + 1}, device_id_type=MESH)

    for k in range(1, groups):
        pl.semaphore_signal(
            barrier, 1, device_id={"head": lax.rem(mine + k, groups)}, device_id_type=MESH
        )
    peers = jnp.where(me > 0, 1, 0) + jnp.where(me < size - 1, 1, 0) + (groups - 1)
    pl.semaphore_wait(barrier, peers)

    @pl.when(me == 0)
    def _():
        inbox[...] = jnp.zeros_like(inbox)

    def copy(c):
        return pltpu.make_async_remote_copy(
            src_ref=outbox.at[c],
            dst_ref=inbox.at[c],
            send_sem=send_sem.at[c],
            recv_sem=recv_sem.at[c],
            device_id={"seq": me + 1},
            device_id_type=MESH,
        )

    def place(owner, h):
        return pl.ds(pl.multiple_of(owner * width + h * HD, HD), HD)

    def rows_of(owner):
        return pl.ds(pl.multiple_of(owner * own_rows, CH), own_rows)

    def hand_over(h, k):
        to = lax.rem(mine + k, groups)
        return pltpu.make_async_remote_copy(
            src_ref=finished.at[h, rows_of(to), :],
            dst_ref=exchanged.at[:, place(mine, h)],
            send_sem=row_send.at[h, to],
            recv_sem=row_recv.at[h, mine],
            device_id={"head": to},
            device_id_type=MESH,
        )

    def take_over(h, k):
        source = lax.rem(mine + k, groups)
        return pltpu.make_async_remote_copy(
            src_ref=finished.at[h, rows_of(source), :],
            dst_ref=exchanged.at[:, place(source, h)],
            send_sem=row_send.at[h, source],
            recv_sem=row_recv.at[h, source],
            device_id={"head": source},
            device_id_type=MESH,
        )

    for h in range(local_heads):

        def pass_on(m, carry):
            c = h * M + m

            @pl.when(me > 0)
            def _():
                copy(c).wait_recv()

            arrived = inbox[c].astype(jnp.float32)
            current[m] = arrived

            @pl.when(me < size - 1)
            def _():
                outbox[c] = (prod_ref[c] * arrived + mem_ref[c]).astype(jnp.bfloat16)
                copy(c).start()

            return carry

        lax.fori_loop(0, M, pass_on, 0)
        cols = slice(h * HD, (h + 1) * HD)

        def block(b, carry):
            rows = pl.ds(pl.multiple_of(b * CH, CH), CH)
            at = (b * local_heads + h) * 2
            entering = (
                entry_ref[at] * current[chosen[at]] + entry_ref[at + 1] * current[chosen[at + 1]]
            ).astype(jnp.bfloat16)
            carried = jnp.dot(q_ref[rows, cols], entering, preferred_element_type=jnp.float32)
            total = att_ref[rows, cols] + growth_ref[rows, h : h + 1] * carried
            scale = lax.rsqrt(jnp.mean(total * total, axis=-1, keepdims=True) + 1e-06)
            finished[h, rows, :] = (total * scale * gain_ref[:, cols]).astype(jnp.bfloat16)
            return carry

        lax.fori_loop(0, blocks, block, 0, unroll=4)
        for k in range(1, groups):
            hand_over(h, k).start()
        exchanged[:, place(mine, h)] = finished[h, rows_of(mine), :]

    fetch.wait()
    half = local_heads // 2
    tile = out_ref.shape[1] // 4
    for part in range(2):
        for h in range(part * half, (part + 1) * half):
            for k in range(1, groups):
                take_over(h, k).wait_recv()

        def project(n, carry):
            columns = pl.ds(pl.multiple_of(n * tile, HD), tile)
            if part == 0:
                total = jnp.zeros((own_rows, tile), jnp.float32)
            else:
                total = partial[:, columns]
            for source in range(groups):
                begin = source * width + part * half * HD
                depth = slice(begin, begin + half * HD)
                total += jnp.dot(
                    exchanged[:, depth], w_ref[depth, columns], preferred_element_type=jnp.float32
                )
            if part == 0:
                partial[:, columns] = total
            else:
                out_ref[:, columns] = total.astype(jnp.bfloat16)
            return carry

        lax.fori_loop(0, 4, project, 0)

    @pl.when(me < size - 1)
    def _():
        def drain(c, carry):
            copy(c).wait_send()
            return carry

        lax.fori_loop(0, pieces, drain, 0)

    for h in range(local_heads):
        for k in range(1, groups):
            hand_over(h, k).wait_send()


def per_device(
    tokens, w_query, w_key, w_value, w_out, norm_gain, forget_rate, routing, memory_blend_share
):
    tok_rows = tokens.shape[0]
    width = w_query.shape[1]
    local_heads = width // HD
    num_blocks = tok_rows // CH
    groups = lax.axis_size("head")
    own_rows, model = tok_rows // groups, w_out.shape[1]
    pieces = local_heads * M
    whole_out = lax.all_gather(w_out, "head", axis=0, tiled=True)

    def project(weight):
        return jnp.dot(tokens, weight, preferred_element_type=jnp.float32).astype(jnp.bfloat16)

    key_raw, value_rows, query = project(w_key), project(w_value), project(w_query)
    chosen = routing.reshape(-1)
    smem = pl.BlockSpec(memory_space=SMEM)
    vmem = pl.BlockSpec(memory_space=VMEM)
    attended, memory, growth, entry, products = pl.pallas_call(
        local_kernel,
        out_shape=(
            jax.ShapeDtypeStruct((tok_rows, width), jnp.float32),
            jax.ShapeDtypeStruct((pieces, HD, HD), jnp.float32),
            jax.ShapeDtypeStruct((tok_rows, local_heads), jnp.float32),
            jax.ShapeDtypeStruct((num_blocks * local_heads * 2, 1, HD), jnp.float32),
            jax.ShapeDtypeStruct((pieces, 1, HD), jnp.float32),
        ),
        in_specs=[smem] * 2 + [vmem] * 4,
        out_specs=(vmem,) * 5,
        compiler_params=pltpu.CompilerParams(vmem_limit_bytes=LIMIT),
        name="local",
    )(chosen, memory_blend_share.reshape(-1), query, key_raw, value_rows, forget_rate)
    return pl.pallas_call(
        chain_kernel,
        out_shape=jax.ShapeDtypeStruct((own_rows, model), jnp.bfloat16),
        in_specs=[smem] + [vmem] * 7 + [pl.BlockSpec(memory_space=pl.ANY)],
        out_specs=vmem,
        scratch_shapes=[
            VMEM((pieces, HD, HD), jnp.bfloat16),
            VMEM((pieces, HD, HD), jnp.bfloat16),
            VMEM((M, HD, HD), jnp.float32),
            VMEM((local_heads, tok_rows, HD), jnp.bfloat16),
            VMEM((own_rows, groups * width), jnp.bfloat16),
            VMEM((own_rows, model), jnp.float32),
            VMEM((groups * width, model), jnp.bfloat16),
            pltpu.SemaphoreType.DMA,
            pltpu.SemaphoreType.DMA((pieces,)),
            pltpu.SemaphoreType.DMA((pieces,)),
            pltpu.SemaphoreType.DMA((local_heads, groups)),
            pltpu.SemaphoreType.DMA((local_heads, groups)),
        ],
        compiler_params=pltpu.CompilerParams(
            collective_id=0, has_side_effects=True, vmem_limit_bytes=LIMIT
        ),
        name="chain",
    )(chosen, entry, products, memory, query, growth, attended, norm_gain[None], whole_out)


def solution(mesh):
    placed = (
        P("seq", None),
        P(None, "head"),
        P(None, "head"),
        P(None, "head"),
        P("head", None),
        P("head"),
        P("seq", "head"),
        P("seq", "head", None),
        P("seq", "head", None),
    )
    return jax.shard_map(
        per_device, mesh=mesh, in_specs=placed, out_specs=P(("seq", "head"), None), check_vma=False
    )
```

```python
import jax
import jax.numpy as jnp
from jax import lax
from jax.experimental import pallas as pl
from jax.experimental.pallas import tpu as pltpu
from jax.sharding import PartitionSpec as P

HD = 128
M = 8
CH = 64

HIGH = lax.Precision.HIGHEST
MESH = pl.DeviceIdType.MESH
VMEM = pltpu.VMEM
SMEM = pltpu.SMEM
LIMIT = 60 * 1024 * 1024


def local_kernel(
    chosen, shares, q_ref, k_ref, v_ref, rate_ref, att_ref, mem_ref, growth_ref, entry_ref, prod_ref
):
    tok_rows, local_heads = rate_ref.shape
    blocks = tok_rows // CH
    mem_ref[...] = jnp.zeros_like(mem_ref)
    prod_ref[...] = jnp.ones_like(prod_ref)
    t = lax.broadcasted_iota(jnp.int32, (CH, CH), 0)
    s = lax.broadcasted_iota(jnp.int32, (CH, CH), 1)
    causal = t >= s

    def block(b, carry):
        rows = pl.ds(pl.multiple_of(b * CH, CH), CH)
        rates = rate_ref[rows, :]
        columns = -jnp.dot(
            jnp.where(t >= s, 1.0, 0.0), rates, precision=HIGH, preferred_element_type=jnp.float32
        )
        lines = -lax.dot_general(
            rates,
            jnp.where(t <= s, 1.0, 0.0),
            (((0,), (0,)), ((), ())),
            precision=HIGH,
            preferred_element_type=jnp.float32,
        )
        growths = jnp.exp(columns)
        growth_ref[rows, :] = growths
        for h in range(local_heads):
            cols = slice(h * HD, (h + 1) * HD)
            query = q_ref[rows, cols]
            wide = k_ref[rows, cols].astype(jnp.float32)
            values = v_ref[rows, cols]
            keys = wide * lax.rsqrt(jnp.sum(wide * wide, axis=-1, keepdims=True) + 1e-06)
            keys = keys.astype(jnp.bfloat16)
            column = columns[:, h : h + 1]
            line = lines[h : h + 1, :]
            gaps = jnp.where(causal, column - line, 0.0)
            decays = jnp.where(causal, jnp.exp(gaps), 0.0)
            scores = lax.dot_general(
                query, keys, (((1,), (1,)), ((), ())), preferred_element_type=jnp.float32
            )
            weighted = (scores * decays).astype(jnp.bfloat16)
            within = jnp.dot(weighted, values, preferred_element_type=jnp.float32)
            ending = column[CH - 1 : CH]
            scaled = (keys.astype(jnp.float32) * jnp.exp(ending - column)).astype(jnp.bfloat16)
            written = lax.dot_general(
                scaled, values, (((0,), (0,)), ((), ())), preferred_element_type=jnp.float32
            )
            at = (b * local_heads + h) * 2
            first, second = h * M + chosen[at], h * M + chosen[at + 1]
            share_a, share_b = shares[at], shares[at + 1]
            fade = jnp.broadcast_to(growths[CH - 1 : CH, h : h + 1], (1, HD))
            old_a = mem_ref[first]
            old_b = mem_ref[second]
            mixed = (share_a * old_a + share_b * old_b).astype(jnp.bfloat16)
            carried = jnp.dot(query, mixed, preferred_element_type=jnp.float32)
            att_ref[rows, cols] = (
                growths[:, h : h + 1] * carried + (share_a + share_b) * within
            )
            mem_ref[first] = fade * old_a + written
            mem_ref[second] = fade * old_b + written
            prod_a, prod_b = prod_ref[first], prod_ref[second]
            entry_ref[at] = share_a * prod_a
            entry_ref[at + 1] = share_b * prod_b
            prod_ref[first] = fade * prod_a
            prod_ref[second] = fade * prod_b
        return carry

    lax.fori_loop(0, blocks, block, 0)


def chain_kernel(
    chosen,
    entry_ref,
    prod_ref,
    mem_ref,
    q_ref,
    growth_ref,
    att_ref,
    gain_ref,
    exchanged,
    inbox,
    outbox,
    current,
    finished,
    send_sem,
    recv_sem,
    row_send,
    row_recv,
):
    size, me = lax.axis_size("seq"), lax.axis_index("seq")
    groups, mine = lax.axis_size("head"), lax.axis_index("head")
    pieces = mem_ref.shape[0]
    local_heads = pieces // M
    width = local_heads * HD
    blocks = q_ref.shape[0] // CH
    own_rows = q_ref.shape[0] // groups
    barrier = pltpu.get_barrier_semaphore()

    @pl.when(me > 0)
    def _():
        pl.semaphore_signal(barrier, 1, device_id={"seq": me - 1}, device_id_type=MESH)

    @pl.when(me < size - 1)
    def _():
        pl.semaphore_signal(barrier, 1, device_id={"seq": me + 1}, device_id_type=MESH)

    for k in range(1, groups):
        pl.semaphore_signal(
            barrier, 1, device_id={"head": lax.rem(mine + k, groups)}, device_id_type=MESH
        )
    peers = jnp.where(me > 0, 1, 0) + jnp.where(me < size - 1, 1, 0) + (groups - 1)
    pl.semaphore_wait(barrier, peers)

    @pl.when(me == 0)
    def _():
        inbox[...] = jnp.zeros_like(inbox)

    def copy(c):
        return pltpu.make_async_remote_copy(
            src_ref=outbox.at[c],
            dst_ref=inbox.at[c],
            send_sem=send_sem.at[c],
            recv_sem=recv_sem.at[c],
            device_id={"seq": me + 1},
            device_id_type=MESH,
        )

    def place(owner, h):
        return pl.ds(pl.multiple_of(owner * width + h * HD, HD), HD)

    def rows_of(owner):
        return pl.ds(pl.multiple_of(owner * own_rows, CH), own_rows)

    def hand_over(h, k):
        to = lax.rem(mine + k, groups)
        return pltpu.make_async_remote_copy(
            src_ref=finished.at[h, rows_of(to), :],
            dst_ref=exchanged.at[:, place(mine, h)],
            send_sem=row_send.at[h, to],
            recv_sem=row_recv.at[h, mine],
            device_id={"head": to},
            device_id_type=MESH,
        )

    def take_over(h, k):
        source = lax.rem(mine + k, groups)
        return pltpu.make_async_remote_copy(
            src_ref=finished.at[h, rows_of(source), :],
            dst_ref=exchanged.at[:, place(source, h)],
            send_sem=row_send.at[h, source],
            recv_sem=row_recv.at[h, source],
            device_id={"head": source},
            device_id_type=MESH,
        )

    for h in range(local_heads):

        def pass_on(m, carry):
            c = h * M + m

            @pl.when(me > 0)
            def _():
                copy(c).wait_recv()

            arrived = inbox[c].astype(jnp.float32)
            current[m] = arrived

            @pl.when(me < size - 1)
            def _():
                outbox[c] = (prod_ref[c] * arrived + mem_ref[c]).astype(jnp.bfloat16)
                copy(c).start()

            return carry

        lax.fori_loop(0, M, pass_on, 0)
        cols = slice(h * HD, (h + 1) * HD)

        def block(b, carry):
            rows = pl.ds(pl.multiple_of(b * CH, CH), CH)
            at = (b * local_heads + h) * 2
            entering = (
                entry_ref[at] * current[chosen[at]] + entry_ref[at + 1] * current[chosen[at + 1]]
            ).astype(jnp.bfloat16)
            carried = jnp.dot(q_ref[rows, cols], entering, preferred_element_type=jnp.float32)
            total = att_ref[rows, cols] + growth_ref[rows, h : h + 1] * carried
            scale = lax.rsqrt(jnp.mean(total * total, axis=-1, keepdims=True) + 1e-06)
            finished[h, rows, :] = (total * scale * gain_ref[:, cols]).astype(jnp.bfloat16)
            return carry

        lax.fori_loop(0, blocks, block, 0, unroll=4)
        for k in range(1, groups):
            hand_over(h, k).start()
        exchanged[:, place(mine, h)] = finished[h, rows_of(mine), :]

    for h in range(local_heads):
        for k in range(1, groups):
            take_over(h, k).wait_recv()

    @pl.when(me < size - 1)
    def _():
        def drain(c, carry):
            copy(c).wait_send()
            return carry

        lax.fori_loop(0, pieces, drain, 0)

    for h in range(local_heads):
        for k in range(1, groups):
            hand_over(h, k).wait_send()


def per_device(
    tokens, w_query, w_key, w_value, w_out, norm_gain, forget_rate, routing, memory_blend_share
):
    tok_rows = tokens.shape[0]
    width = w_query.shape[1]
    local_heads = width // HD
    num_blocks = tok_rows // CH
    groups = lax.axis_size("head")
    own_rows = tok_rows // groups
    pieces = local_heads * M
    whole_out = lax.all_gather(w_out, "head", axis=0, tiled=True)

    def project(weight):
        return jnp.dot(tokens, weight, preferred_element_type=jnp.float32).astype(jnp.bfloat16)

    key_raw, value_rows, query = project(w_key), project(w_value), project(w_query)
    chosen = routing.reshape(-1)
    smem = pl.BlockSpec(memory_space=SMEM)
    vmem = pl.BlockSpec(memory_space=VMEM)
    attended, memory, growth, entry, products = pl.pallas_call(
        local_kernel,
        out_shape=(
            jax.ShapeDtypeStruct((tok_rows, width), jnp.float32),
            jax.ShapeDtypeStruct((pieces, HD, HD), jnp.float32),
            jax.ShapeDtypeStruct((tok_rows, local_heads), jnp.float32),
            jax.ShapeDtypeStruct((num_blocks * local_heads * 2, 1, HD), jnp.float32),
            jax.ShapeDtypeStruct((pieces, 1, HD), jnp.float32),
        ),
        in_specs=[smem] * 2 + [vmem] * 4,
        out_specs=(vmem,) * 5,
        compiler_params=pltpu.CompilerParams(vmem_limit_bytes=LIMIT),
        name="local",
    )(chosen, memory_blend_share.reshape(-1), query, key_raw, value_rows, forget_rate)
    exchanged = pl.pallas_call(
        chain_kernel,
        out_shape=jax.ShapeDtypeStruct((own_rows, groups * width), jnp.bfloat16),
        in_specs=[smem] + [vmem] * 7,
        out_specs=vmem,
        scratch_shapes=[
            VMEM((pieces, HD, HD), jnp.bfloat16),
            VMEM((pieces, HD, HD), jnp.bfloat16),
            VMEM((M, HD, HD), jnp.float32),
            VMEM((local_heads, tok_rows, HD), jnp.bfloat16),
            pltpu.SemaphoreType.DMA((pieces,)),
            pltpu.SemaphoreType.DMA((pieces,)),
            pltpu.SemaphoreType.DMA((local_heads, groups)),
            pltpu.SemaphoreType.DMA((local_heads, groups)),
        ],
        compiler_params=pltpu.CompilerParams(
            collective_id=0, has_side_effects=True, vmem_limit_bytes=LIMIT
        ),
        name="chain",
    )(chosen, entry, products, memory, query, growth, attended, norm_gain[None])
    result = jnp.dot(exchanged, whole_out, preferred_element_type=jnp.float32)
    return result.astype(jnp.bfloat16)


def solution(mesh):
    placed = (
        P("seq", None),
        P(None, "head"),
        P(None, "head"),
        P(None, "head"),
        P("head", None),
        P("head"),
        P("seq", "head"),
        P("seq", "head", None),
        P("seq", "head", None),
    )
    return jax.shard_map(
        per_device, mesh=mesh, in_specs=placed, out_specs=P(("seq", "head"), None), check_vma=False
    )
```

```python
import jax
import jax.numpy as jnp
from jax import lax
from jax.experimental import pallas as pl
from jax.experimental.pallas import tpu as pltpu
from jax.sharding import PartitionSpec as P

HD = 128
M = 8
CH = 64

HIGH = lax.Precision.HIGHEST
MESH = pl.DeviceIdType.MESH
VMEM = pltpu.VMEM
SMEM = pltpu.SMEM
PARTS = 4
LIMIT = 60 * 1024 * 1024


def local_kernel(
    chosen, shares, q_ref, k_ref, v_ref, rate_ref, att_ref, mem_ref, growth_ref, entry_ref, prod_ref
):
    tok_rows, local_heads = rate_ref.shape
    blocks = tok_rows // CH
    mem_ref[...] = jnp.zeros_like(mem_ref)
    prod_ref[...] = jnp.ones_like(prod_ref)
    t = lax.broadcasted_iota(jnp.int32, (CH, CH), 0)
    s = lax.broadcasted_iota(jnp.int32, (CH, CH), 1)
    causal = t >= s

    def block(b, carry):
        rows = pl.ds(pl.multiple_of(b * CH, CH), CH)
        rates = rate_ref[rows, :]
        columns = -jnp.dot(
            jnp.where(t >= s, 1.0, 0.0), rates, precision=HIGH, preferred_element_type=jnp.float32
        )
        lines = -lax.dot_general(
            rates,
            jnp.where(t <= s, 1.0, 0.0),
            (((0,), (0,)), ((), ())),
            precision=HIGH,
            preferred_element_type=jnp.float32,
        )
        growths = jnp.exp(columns)
        growth_ref[rows, :] = growths
        for h in range(local_heads):
            cols = slice(h * HD, (h + 1) * HD)
            query = q_ref[rows, cols]
            wide = k_ref[rows, cols].astype(jnp.float32)
            values = v_ref[rows, cols]
            keys = wide * lax.rsqrt(jnp.sum(wide * wide, axis=-1, keepdims=True) + 1e-06)
            keys = keys.astype(jnp.bfloat16)
            column = columns[:, h : h + 1]
            line = lines[h : h + 1, :]
            gaps = jnp.where(causal, column - line, 0.0)
            decays = jnp.where(causal, jnp.exp(gaps), 0.0)
            scores = lax.dot_general(
                query, keys, (((1,), (1,)), ((), ())), preferred_element_type=jnp.float32
            )
            weighted = (scores * decays).astype(jnp.bfloat16)
            within = jnp.dot(weighted, values, preferred_element_type=jnp.float32)
            ending = column[CH - 1 : CH]
            scaled = (keys.astype(jnp.float32) * jnp.exp(ending - column)).astype(jnp.bfloat16)
            written = lax.dot_general(
                scaled, values, (((0,), (0,)), ((), ())), preferred_element_type=jnp.float32
            )
            at = (b * local_heads + h) * 2
            first, second = h * M + chosen[at], h * M + chosen[at + 1]
            share_a, share_b = shares[at], shares[at + 1]
            fade = jnp.broadcast_to(growths[CH - 1 : CH, h : h + 1], (1, HD))
            old_a = mem_ref[first]
            old_b = mem_ref[second]
            mixed = (share_a * old_a + share_b * old_b).astype(jnp.bfloat16)
            carried = jnp.dot(query, mixed, preferred_element_type=jnp.float32)
            att_ref[rows, cols] = (
                growths[:, h : h + 1] * carried + (share_a + share_b) * within
            )
            mem_ref[first] = fade * old_a + written
            mem_ref[second] = fade * old_b + written
            prod_a, prod_b = prod_ref[first], prod_ref[second]
            entry_ref[at] = share_a * prod_a
            entry_ref[at + 1] = share_b * prod_b
            prod_ref[first] = fade * prod_a
            prod_ref[second] = fade * prod_b
        return carry

    lax.fori_loop(0, blocks, block, 0)


def weights_of(owner, depth):
    return pl.ds(pl.multiple_of(owner * depth, depth), depth)


def chain_kernel(
    chosen,
    entry_ref,
    prod_ref,
    mem_ref,
    q_ref,
    growth_ref,
    att_ref,
    gain_ref,
    w_ref,
    exchanged,
    gathered,
    inbox,
    outbox,
    current,
    finished,
    send_sem,
    recv_sem,
    row_send,
    row_recv,
    own_sem,
    near_send,
    near_recv,
    pass_send,
    pass_recv,
):
    size, me = lax.axis_size("seq"), lax.axis_index("seq")
    groups, mine = lax.axis_size("head"), lax.axis_index("head")
    pieces = mem_ref.shape[0]
    local_heads = pieces // M
    width = local_heads * HD
    blocks = q_ref.shape[0] // CH
    own_rows = q_ref.shape[0] // groups
    barrier = pltpu.get_barrier_semaphore()

    @pl.when(me > 0)
    def _():
        pl.semaphore_signal(barrier, 1, device_id={"seq": me - 1}, device_id_type=MESH)

    @pl.when(me < size - 1)
    def _():
        pl.semaphore_signal(barrier, 1, device_id={"seq": me + 1}, device_id_type=MESH)

    for k in range(1, groups):
        pl.semaphore_signal(
            barrier, 1, device_id={"head": lax.rem(mine + k, groups)}, device_id_type=MESH
        )
    peers = jnp.where(me > 0, 1, 0) + jnp.where(me < size - 1, 1, 0) + (groups - 1)
    pl.semaphore_wait(barrier, peers)

    @pl.when(me == 0)
    def _():
        inbox[...] = jnp.zeros_like(inbox)

    def copy(c):
        return pltpu.make_async_remote_copy(
            src_ref=outbox.at[c],
            dst_ref=inbox.at[c],
            send_sem=send_sem.at[c],
            recv_sem=recv_sem.at[c],
            device_id={"seq": me + 1},
            device_id_type=MESH,
        )

    def place(owner, h):
        return pl.ds(pl.multiple_of(owner * width + h * HD, HD), HD)

    def rows_of(owner):
        return pl.ds(pl.multiple_of(owner * own_rows, CH), own_rows)

    def hand_over(h, k):
        to = lax.rem(mine + k, groups)
        return pltpu.make_async_remote_copy(
            src_ref=finished.at[h, rows_of(to), :],
            dst_ref=exchanged.at[:, place(mine, h)],
            send_sem=row_send.at[h, to],
            recv_sem=row_recv.at[h, mine],
            device_id={"head": to},
            device_id_type=MESH,
        )

    def take_over(h, k):
        source = lax.rem(mine + k, groups)
        return pltpu.make_async_remote_copy(
            src_ref=finished.at[h, rows_of(source), :],
            dst_ref=exchanged.at[:, place(source, h)],
            send_sem=row_send.at[h, source],
            recv_sem=row_recv.at[h, source],
            device_id={"head": source},
            device_id_type=MESH,
        )

    twin = mine + 1 - 2 * lax.rem(mine, 2)
    depth = w_ref.shape[0]
    piece = depth // PARTS

    def weights(owner, part):
        return pl.ds(pl.multiple_of(owner * depth + part * piece, piece), piece)

    def share(k, part):
        to = twin if k == 0 else lax.rem(mine + 2 * k, groups)
        return pltpu.make_async_remote_copy(
            src_ref=w_ref.at[part * piece : (part + 1) * piece, :],
            dst_ref=gathered.at[weights(mine, part), :],
            send_sem=near_send.at[k, part],
            recv_sem=near_recv.at[k, part],
            device_id={"head": to},
            device_id_type=MESH,
        )

    def relay(k, part):
        source = lax.rem(mine + groups - 2 * k, groups)
        return pltpu.make_async_remote_copy(
            src_ref=gathered.at[weights(source, part), :],
            dst_ref=gathered.at[weights(source, part), :],
            send_sem=pass_send.at[k, part],
            recv_sem=pass_recv.at[k, part],
            device_id={"head": twin},
            device_id_type=MESH,
        )

    keep = pltpu.make_async_copy(w_ref, gathered.at[weights_of(mine, depth), :], own_sem)
    keep.start()
    for part in range(PARTS):
        for k in range(1, groups // 2):
            share(k, part).start()
    for part in range(PARTS):
        share(0, part).start()

    for h in range(local_heads):

        def pass_on(m, carry):
            c = h * M + m

            @pl.when(me > 0)
            def _():
                copy(c).wait_recv()

            arrived = inbox[c].astype(jnp.float32)
            current[m] = arrived

            @pl.when(me < size - 1)
            def _():
                outbox[c] = (prod_ref[c] * arrived + mem_ref[c]).astype(jnp.bfloat16)
                copy(c).start()

            return carry

        lax.fori_loop(0, M, pass_on, 0)
        cols = slice(h * HD, (h + 1) * HD)

        def block(b, carry):
            rows = pl.ds(pl.multiple_of(b * CH, CH), CH)
            at = (b * local_heads + h) * 2
            entering = (
                entry_ref[at] * current[chosen[at]] + entry_ref[at + 1] * current[chosen[at + 1]]
            ).astype(jnp.bfloat16)
            carried = jnp.dot(q_ref[rows, cols], entering, preferred_element_type=jnp.float32)
            total = att_ref[rows, cols] + growth_ref[rows, h : h + 1] * carried
            scale = lax.rsqrt(jnp.mean(total * total, axis=-1, keepdims=True) + 1e-06)
            finished[h, rows, :] = (total * scale * gain_ref[:, cols]).astype(jnp.bfloat16)
            return carry

        lax.fori_loop(0, blocks, block, 0, unroll=4)
        for k in range(1, groups):
            hand_over(h, k).start()
        exchanged[:, place(mine, h)] = finished[h, rows_of(mine), :]

    for part in range(PARTS):
        for k in range(1, groups // 2):
            share(k, part).wait_recv()
            relay(k, part).start()

    for h in range(local_heads):
        for k in range(1, groups):
            take_over(h, k).wait_recv()

    keep.wait()
    for part in range(PARTS):
        share(0, part).wait_recv()
        for k in range(1, groups // 2):
            relay(k, part).wait_recv()
            relay(k, part).wait_send()
        for k in range(groups // 2):
            share(k, part).wait_send()

    @pl.when(me < size - 1)
    def _():
        def drain(c, carry):
            copy(c).wait_send()
            return carry

        lax.fori_loop(0, pieces, drain, 0)

    for h in range(local_heads):
        for k in range(1, groups):
            hand_over(h, k).wait_send()


def per_device(
    tokens, w_query, w_key, w_value, w_out, norm_gain, forget_rate, routing, memory_blend_share
):
    tok_rows = tokens.shape[0]
    width = w_query.shape[1]
    local_heads = width // HD
    num_blocks = tok_rows // CH
    groups = lax.axis_size("head")
    own_rows = tok_rows // groups
    pieces = local_heads * M

    def project(weight):
        return jnp.dot(tokens, weight, preferred_element_type=jnp.float32).astype(jnp.bfloat16)

    key_raw, value_rows, query = project(w_key), project(w_value), project(w_query)
    chosen = routing.reshape(-1)
    smem = pl.BlockSpec(memory_space=SMEM)
    vmem = pl.BlockSpec(memory_space=VMEM)
    attended, memory, growth, entry, products = pl.pallas_call(
        local_kernel,
        out_shape=(
            jax.ShapeDtypeStruct((tok_rows, width), jnp.float32),
            jax.ShapeDtypeStruct((pieces, HD, HD), jnp.float32),
            jax.ShapeDtypeStruct((tok_rows, local_heads), jnp.float32),
            jax.ShapeDtypeStruct((num_blocks * local_heads * 2, 1, HD), jnp.float32),
            jax.ShapeDtypeStruct((pieces, 1, HD), jnp.float32),
        ),
        in_specs=[smem] * 2 + [vmem] * 4,
        out_specs=(vmem,) * 5,
        compiler_params=pltpu.CompilerParams(vmem_limit_bytes=LIMIT),
        name="local",
    )(chosen, memory_blend_share.reshape(-1), query, key_raw, value_rows, forget_rate)
    exchanged, whole_out = pl.pallas_call(
        chain_kernel,
        out_shape=(
            jax.ShapeDtypeStruct((own_rows, groups * width), jnp.bfloat16),
            jax.ShapeDtypeStruct((groups * w_out.shape[0], w_out.shape[1]), jnp.bfloat16),
        ),
        in_specs=[smem] + [vmem] * 8,
        out_specs=(vmem, pl.BlockSpec(memory_space=pltpu.HBM)),
        scratch_shapes=[
            VMEM((pieces, HD, HD), jnp.bfloat16),
            VMEM((pieces, HD, HD), jnp.bfloat16),
            VMEM((M, HD, HD), jnp.float32),
            VMEM((local_heads, tok_rows, HD), jnp.bfloat16),
            pltpu.SemaphoreType.DMA((pieces,)),
            pltpu.SemaphoreType.DMA((pieces,)),
            pltpu.SemaphoreType.DMA((local_heads, groups)),
            pltpu.SemaphoreType.DMA((local_heads, groups)),
            pltpu.SemaphoreType.DMA,
            pltpu.SemaphoreType.DMA((groups // 2, PARTS)),
            pltpu.SemaphoreType.DMA((groups // 2, PARTS)),
            pltpu.SemaphoreType.DMA((groups // 2, PARTS)),
            pltpu.SemaphoreType.DMA((groups // 2, PARTS)),
        ],
        compiler_params=pltpu.CompilerParams(
            collective_id=0, has_side_effects=True, vmem_limit_bytes=LIMIT
        ),
        name="chain",
    )(chosen, entry, products, memory, query, growth, attended, norm_gain[None], w_out)
    result = jnp.dot(exchanged, whole_out, preferred_element_type=jnp.float32)
    return result.astype(jnp.bfloat16)


def solution(mesh):
    placed = (
        P("seq", None),
        P(None, "head"),
        P(None, "head"),
        P(None, "head"),
        P("head", None),
        P("head"),
        P("seq", "head"),
        P("seq", "head", None),
        P("seq", "head", None),
    )
    return jax.shard_map(
        per_device, mesh=mesh, in_specs=placed, out_specs=P(("seq", "head"), None), check_vma=False
    )
```

```python
import jax
import jax.numpy as jnp
from jax import lax
from jax.experimental import pallas as pl
from jax.experimental.pallas import tpu as pltpu
from jax.sharding import PartitionSpec as P

HD = 128
M = 8
CH = 64

HIGH = lax.Precision.HIGHEST
MESH = pl.DeviceIdType.MESH
VMEM = pltpu.VMEM
SMEM = pltpu.SMEM
PARTS = 4
LIMIT = 60 * 1024 * 1024


def local_kernel(
    chosen,
    shares,
    k_ref,
    v_ref,
    rate_ref,
    key_ref,
    state_ref,
    mem_ref,
    column_ref,
    line_ref,
    entry_ref,
    prod_ref,
):
    tok_rows, local_heads = rate_ref.shape
    blocks = tok_rows // CH
    mem_ref[...] = jnp.zeros_like(mem_ref)
    prod_ref[...] = jnp.ones_like(prod_ref)
    t = lax.broadcasted_iota(jnp.int32, (CH, CH), 0)
    s = lax.broadcasted_iota(jnp.int32, (CH, CH), 1)

    def block(b, carry):
        rows = pl.ds(pl.multiple_of(b * CH, CH), CH)
        rates = rate_ref[rows, :]
        columns = -jnp.dot(
            jnp.where(t >= s, 1.0, 0.0), rates, precision=HIGH, preferred_element_type=jnp.float32
        )
        lines = -lax.dot_general(
            rates,
            jnp.where(t <= s, 1.0, 0.0),
            (((0,), (0,)), ((), ())),
            precision=HIGH,
            preferred_element_type=jnp.float32,
        )
        growths = jnp.exp(columns)
        column_ref[rows, :] = columns
        line_ref[b] = lines
        for h in range(local_heads):
            cols = slice(h * HD, (h + 1) * HD)
            wide = k_ref[rows, cols].astype(jnp.float32)
            values = v_ref[rows, cols]
            keys = wide * lax.rsqrt(jnp.sum(wide * wide, axis=-1, keepdims=True) + 1e-06)
            keys = keys.astype(jnp.bfloat16)
            key_ref[rows, cols] = keys
            column = columns[:, h : h + 1]
            ending = column[CH - 1 : CH]
            scaled = (keys.astype(jnp.float32) * jnp.exp(ending - column)).astype(jnp.bfloat16)
            written = lax.dot_general(
                scaled, values, (((0,), (0,)), ((), ())), preferred_element_type=jnp.float32
            )
            at = (b * local_heads + h) * 2
            first, second = h * M + chosen[at], h * M + chosen[at + 1]
            share_a, share_b = shares[at], shares[at + 1]
            fade = jnp.broadcast_to(growths[CH - 1 : CH, h : h + 1], (1, HD))
            old_a = mem_ref[first]
            old_b = mem_ref[second]
            state_ref[b * local_heads + h] = (share_a * old_a + share_b * old_b).astype(jnp.bfloat16)
            mem_ref[first] = fade * old_a + written
            mem_ref[second] = fade * old_b + written
            prod_a, prod_b = prod_ref[first], prod_ref[second]
            entry_ref[at] = share_a * prod_a
            entry_ref[at + 1] = share_b * prod_b
            prod_ref[first] = fade * prod_a
            prod_ref[second] = fade * prod_b
        return carry

    lax.fori_loop(0, blocks, block, 0)


def weights_of(owner, depth):
    return pl.ds(pl.multiple_of(owner * depth, depth), depth)


def chain_kernel(
    chosen,
    shares,
    entry_ref,
    prod_ref,
    mem_ref,
    q_ref,
    key_ref,
    v_ref,
    column_ref,
    line_ref,
    state_ref,
    gain_ref,
    w_ref,
    exchanged,
    gathered,
    inbox,
    outbox,
    current,
    finished,
    send_sem,
    recv_sem,
    row_send,
    row_recv,
    own_sem,
    near_send,
    near_recv,
    pass_send,
    pass_recv,
):
    size, me = lax.axis_size("seq"), lax.axis_index("seq")
    groups, mine = lax.axis_size("head"), lax.axis_index("head")
    pieces = mem_ref.shape[0]
    local_heads = pieces // M
    width = local_heads * HD
    blocks = q_ref.shape[0] // CH
    own_rows = q_ref.shape[0] // groups
    barrier = pltpu.get_barrier_semaphore()

    @pl.when(me > 0)
    def _():
        pl.semaphore_signal(barrier, 1, device_id={"seq": me - 1}, device_id_type=MESH)

    @pl.when(me < size - 1)
    def _():
        pl.semaphore_signal(barrier, 1, device_id={"seq": me + 1}, device_id_type=MESH)

    for k in range(1, groups):
        pl.semaphore_signal(
            barrier, 1, device_id={"head": lax.rem(mine + k, groups)}, device_id_type=MESH
        )
    peers = jnp.where(me > 0, 1, 0) + jnp.where(me < size - 1, 1, 0) + (groups - 1)
    pl.semaphore_wait(barrier, peers)

    @pl.when(me == 0)
    def _():
        inbox[...] = jnp.zeros_like(inbox)

    def copy(c):
        return pltpu.make_async_remote_copy(
            src_ref=outbox.at[c],
            dst_ref=inbox.at[c],
            send_sem=send_sem.at[c],
            recv_sem=recv_sem.at[c],
            device_id={"seq": me + 1},
            device_id_type=MESH,
        )

    def place(owner, h):
        return pl.ds(pl.multiple_of(owner * width + h * HD, HD), HD)

    def rows_of(owner):
        return pl.ds(pl.multiple_of(owner * own_rows, CH), own_rows)

    def hand_over(h, k):
        to = lax.rem(mine + k, groups)
        return pltpu.make_async_remote_copy(
            src_ref=finished.at[h, rows_of(to), :],
            dst_ref=exchanged.at[:, place(mine, h)],
            send_sem=row_send.at[h, to],
            recv_sem=row_recv.at[h, mine],
            device_id={"head": to},
            device_id_type=MESH,
        )

    def take_over(h, k):
        source = lax.rem(mine + k, groups)
        return pltpu.make_async_remote_copy(
            src_ref=finished.at[h, rows_of(source), :],
            dst_ref=exchanged.at[:, place(source, h)],
            send_sem=row_send.at[h, source],
            recv_sem=row_recv.at[h, source],
            device_id={"head": source},
            device_id_type=MESH,
        )

    t = lax.broadcasted_iota(jnp.int32, (CH, CH), 0)
    s = lax.broadcasted_iota(jnp.int32, (CH, CH), 1)
    causal = t >= s
    twin = mine + 1 - 2 * lax.rem(mine, 2)
    depth = w_ref.shape[0]
    piece = depth // PARTS

    def weights(owner, part):
        return pl.ds(pl.multiple_of(owner * depth + part * piece, piece), piece)

    def share(k, part):
        to = twin if k == 0 else lax.rem(mine + 2 * k, groups)
        return pltpu.make_async_remote_copy(
            src_ref=w_ref.at[part * piece : (part + 1) * piece, :],
            dst_ref=gathered.at[weights(mine, part), :],
            send_sem=near_send.at[k, part],
            recv_sem=near_recv.at[k, part],
            device_id={"head": to},
            device_id_type=MESH,
        )

    def relay(k, part):
        source = lax.rem(mine + groups - 2 * k, groups)
        return pltpu.make_async_remote_copy(
            src_ref=gathered.at[weights(source, part), :],
            dst_ref=gathered.at[weights(source, part), :],
            send_sem=pass_send.at[k, part],
            recv_sem=pass_recv.at[k, part],
            device_id={"head": twin},
            device_id_type=MESH,
        )

    keep = pltpu.make_async_copy(w_ref, gathered.at[weights_of(mine, depth), :], own_sem)
    keep.start()
    for part in range(PARTS):
        for k in range(1, groups // 2):
            share(k, part).start()
    for part in range(PARTS):
        share(0, part).start()

    for h in range(local_heads):

        def pass_on(m, carry):
            c = h * M + m

            @pl.when(me > 0)
            def _():
                copy(c).wait_recv()

            arrived = inbox[c].astype(jnp.float32)
            current[m] = arrived

            @pl.when(me < size - 1)
            def _():
                outbox[c] = (prod_ref[c] * arrived + mem_ref[c]).astype(jnp.bfloat16)
                copy(c).start()

            return carry

        lax.fori_loop(0, M, pass_on, 0)
        cols = slice(h * HD, (h + 1) * HD)

        def block(b, carry):
            rows = pl.ds(pl.multiple_of(b * CH, CH), CH)
            at = (b * local_heads + h) * 2
            entering = (
                state_ref[b * local_heads + h].astype(jnp.float32)
                + entry_ref[at] * current[chosen[at]]
                + entry_ref[at + 1] * current[chosen[at + 1]]
            ).astype(jnp.bfloat16)
            query, keys, values = q_ref[rows, cols], key_ref[rows, cols], v_ref[rows, cols]
            column = column_ref[rows, h : h + 1]
            line = line_ref[b, h : h + 1, :]
            gaps = jnp.where(causal, column - line, 0.0)
            decays = jnp.where(causal, jnp.exp(gaps), 0.0)
            scores = lax.dot_general(
                query, keys, (((1,), (1,)), ((), ())), preferred_element_type=jnp.float32
            )
            weighted = (scores * decays).astype(jnp.bfloat16)
            within = jnp.dot(weighted, values, preferred_element_type=jnp.float32)
            carried = jnp.dot(query, entering, preferred_element_type=jnp.float32)
            total = jnp.exp(column) * carried + (shares[at] + shares[at + 1]) * within
            scale = lax.rsqrt(jnp.mean(total * total, axis=-1, keepdims=True) + 1e-06)
            finished[h, rows, :] = (total * scale * gain_ref[:, cols]).astype(jnp.bfloat16)
            return carry

        lax.fori_loop(0, blocks, block, 0, unroll=4)
        for k in range(1, groups):
            hand_over(h, k).start()
        exchanged[:, place(mine, h)] = finished[h, rows_of(mine), :]

    for part in range(PARTS):
        for k in range(1, groups // 2):
            share(k, part).wait_recv()
            relay(k, part).start()

    for h in range(local_heads):
        for k in range(1, groups):
            take_over(h, k).wait_recv()

    keep.wait()
    for part in range(PARTS):
        share(0, part).wait_recv()
        for k in range(1, groups // 2):
            relay(k, part).wait_recv()
            relay(k, part).wait_send()
        for k in range(groups // 2):
            share(k, part).wait_send()

    @pl.when(me < size - 1)
    def _():
        def drain(c, carry):
            copy(c).wait_send()
            return carry

        lax.fori_loop(0, pieces, drain, 0)

    for h in range(local_heads):
        for k in range(1, groups):
            hand_over(h, k).wait_send()


def per_device(
    tokens, w_query, w_key, w_value, w_out, norm_gain, forget_rate, routing, memory_blend_share
):
    tok_rows = tokens.shape[0]
    width = w_query.shape[1]
    local_heads = width // HD
    num_blocks = tok_rows // CH
    groups = lax.axis_size("head")
    own_rows = tok_rows // groups
    pieces = local_heads * M

    def project(weight):
        return jnp.dot(tokens, weight, preferred_element_type=jnp.float32).astype(jnp.bfloat16)

    key_raw, value_rows, query = project(w_key), project(w_value), project(w_query)
    chosen, shares = routing.reshape(-1), memory_blend_share.reshape(-1)
    smem = pl.BlockSpec(memory_space=SMEM)
    vmem = pl.BlockSpec(memory_space=VMEM)
    keys, states, memory, columns, lines, entry, products = pl.pallas_call(
        local_kernel,
        out_shape=(
            jax.ShapeDtypeStruct((tok_rows, width), jnp.bfloat16),
            jax.ShapeDtypeStruct((num_blocks * local_heads, HD, HD), jnp.bfloat16),
            jax.ShapeDtypeStruct((pieces, HD, HD), jnp.float32),
            jax.ShapeDtypeStruct((tok_rows, local_heads), jnp.float32),
            jax.ShapeDtypeStruct((num_blocks, local_heads, CH), jnp.float32),
            jax.ShapeDtypeStruct((num_blocks * local_heads * 2, 1, HD), jnp.float32),
            jax.ShapeDtypeStruct((pieces, 1, HD), jnp.float32),
        ),
        in_specs=[smem] * 2 + [vmem] * 3,
        out_specs=(vmem,) * 7,
        compiler_params=pltpu.CompilerParams(vmem_limit_bytes=LIMIT),
        name="local",
    )(chosen, shares, key_raw, value_rows, forget_rate)
    exchanged, whole_out = pl.pallas_call(
        chain_kernel,
        out_shape=(
            jax.ShapeDtypeStruct((own_rows, groups * width), jnp.bfloat16),
            jax.ShapeDtypeStruct((groups * w_out.shape[0], w_out.shape[1]), jnp.bfloat16),
        ),
        in_specs=[smem] * 2 + [vmem] * 11,
        out_specs=(vmem, pl.BlockSpec(memory_space=pltpu.HBM)),
        scratch_shapes=[
            VMEM((pieces, HD, HD), jnp.bfloat16),
            VMEM((pieces, HD, HD), jnp.bfloat16),
            VMEM((M, HD, HD), jnp.float32),
            VMEM((local_heads, tok_rows, HD), jnp.bfloat16),
            pltpu.SemaphoreType.DMA((pieces,)),
            pltpu.SemaphoreType.DMA((pieces,)),
            pltpu.SemaphoreType.DMA((local_heads, groups)),
            pltpu.SemaphoreType.DMA((local_heads, groups)),
            pltpu.SemaphoreType.DMA,
            pltpu.SemaphoreType.DMA((groups // 2, PARTS)),
            pltpu.SemaphoreType.DMA((groups // 2, PARTS)),
            pltpu.SemaphoreType.DMA((groups // 2, PARTS)),
            pltpu.SemaphoreType.DMA((groups // 2, PARTS)),
        ],
        compiler_params=pltpu.CompilerParams(
            collective_id=0, has_side_effects=True, vmem_limit_bytes=LIMIT
        ),
        name="chain",
    )(
        chosen,
        shares,
        entry,
        products,
        memory,
        query,
        keys,
        value_rows,
        columns,
        lines,
        states,
        norm_gain[None],
        w_out,
    )
    result = jnp.dot(exchanged, whole_out, preferred_element_type=jnp.float32)
    return result.astype(jnp.bfloat16)


def solution(mesh):
    placed = (
        P("seq", None),
        P(None, "head"),
        P(None, "head"),
        P(None, "head"),
        P("head", None),
        P("head"),
        P("seq", "head"),
        P("seq", "head", None),
        P("seq", "head", None),
    )
    return jax.shard_map(
        per_device, mesh=mesh, in_specs=placed, out_specs=P(("seq", "head"), None), check_vma=False
    )
```

```python
import jax
import jax.numpy as jnp
from jax import lax
from jax.experimental import pallas as pl
from jax.experimental.pallas import tpu as pltpu
from jax.sharding import PartitionSpec as P

HD = 128
M = 8
CH = 64

HIGH = lax.Precision.HIGHEST
MESH = pl.DeviceIdType.MESH
VMEM = pltpu.VMEM
SMEM = pltpu.SMEM
PARTS = 4
LIMIT = 60 * 1024 * 1024


def local_kernel(
    chosen,
    shares,
    k_ref,
    v_ref,
    rate_ref,
    key_ref,
    state_ref,
    mem_ref,
    column_ref,
    line_ref,
    entry_ref,
    prod_ref,
):
    tok_rows, local_heads = rate_ref.shape
    blocks = tok_rows // CH
    mem_ref[...] = jnp.zeros_like(mem_ref)
    prod_ref[...] = jnp.ones_like(prod_ref)
    t = lax.broadcasted_iota(jnp.int32, (CH, CH), 0)
    s = lax.broadcasted_iota(jnp.int32, (CH, CH), 1)

    def block(b, carry):
        rows = pl.ds(pl.multiple_of(b * CH, CH), CH)
        rates = rate_ref[rows, :]
        columns = -jnp.dot(
            jnp.where(t >= s, 1.0, 0.0), rates, precision=HIGH, preferred_element_type=jnp.float32
        )
        lines = -lax.dot_general(
            rates,
            jnp.where(t <= s, 1.0, 0.0),
            (((0,), (0,)), ((), ())),
            precision=HIGH,
            preferred_element_type=jnp.float32,
        )
        growths = jnp.exp(columns)
        column_ref[rows, :] = columns
        line_ref[b] = lines
        for h in range(local_heads):
            cols = slice(h * HD, (h + 1) * HD)
            wide = k_ref[rows, cols].astype(jnp.float32)
            values = v_ref[rows, cols]
            keys = wide * lax.rsqrt(jnp.sum(wide * wide, axis=-1, keepdims=True) + 1e-06)
            keys = keys.astype(jnp.bfloat16)
            key_ref[rows, cols] = keys
            column = columns[:, h : h + 1]
            ending = column[CH - 1 : CH]
            scaled = (keys.astype(jnp.float32) * jnp.exp(ending - column)).astype(jnp.bfloat16)
            written = lax.dot_general(
                scaled, values, (((0,), (0,)), ((), ())), preferred_element_type=jnp.float32
            )
            at = (b * local_heads + h) * 2
            first, second = h * M + chosen[at], h * M + chosen[at + 1]
            share_a, share_b = shares[at], shares[at + 1]
            fade = jnp.broadcast_to(growths[CH - 1 : CH, h : h + 1], (1, HD))
            old_a = mem_ref[first]
            old_b = mem_ref[second]
            state_ref[b * local_heads + h] = (share_a * old_a + share_b * old_b).astype(jnp.bfloat16)
            mem_ref[first] = fade * old_a + written
            mem_ref[second] = fade * old_b + written
            prod_a, prod_b = prod_ref[first], prod_ref[second]
            entry_ref[at] = share_a * prod_a
            entry_ref[at + 1] = share_b * prod_b
            prod_ref[first] = fade * prod_a
            prod_ref[second] = fade * prod_b
        return carry

    lax.fori_loop(0, blocks, block, 0, unroll=4)


def weights_of(owner, depth):
    return pl.ds(pl.multiple_of(owner * depth, depth), depth)


def chain_kernel(
    chosen,
    shares,
    entry_ref,
    prod_ref,
    mem_ref,
    q_ref,
    key_ref,
    v_ref,
    column_ref,
    line_ref,
    state_ref,
    gain_ref,
    w_ref,
    exchanged,
    gathered,
    inbox,
    outbox,
    current,
    finished,
    send_sem,
    recv_sem,
    row_send,
    row_recv,
    own_sem,
    near_send,
    near_recv,
    pass_send,
    pass_recv,
):
    size, me = lax.axis_size("seq"), lax.axis_index("seq")
    groups, mine = lax.axis_size("head"), lax.axis_index("head")
    pieces = mem_ref.shape[0]
    local_heads = pieces // M
    width = local_heads * HD
    blocks = q_ref.shape[0] // CH
    own_rows = q_ref.shape[0] // groups
    barrier = pltpu.get_barrier_semaphore()

    @pl.when(me > 0)
    def _():
        pl.semaphore_signal(barrier, 1, device_id={"seq": me - 1}, device_id_type=MESH)

    @pl.when(me < size - 1)
    def _():
        pl.semaphore_signal(barrier, 1, device_id={"seq": me + 1}, device_id_type=MESH)

    for k in range(1, groups):
        pl.semaphore_signal(
            barrier, 1, device_id={"head": lax.rem(mine + k, groups)}, device_id_type=MESH
        )
    peers = jnp.where(me > 0, 1, 0) + jnp.where(me < size - 1, 1, 0) + (groups - 1)
    pl.semaphore_wait(barrier, peers)

    @pl.when(me == 0)
    def _():
        inbox[...] = jnp.zeros_like(inbox)

    def copy(c):
        return pltpu.make_async_remote_copy(
            src_ref=outbox.at[c],
            dst_ref=inbox.at[c],
            send_sem=send_sem.at[c],
            recv_sem=recv_sem.at[c],
            device_id={"seq": me + 1},
            device_id_type=MESH,
        )

    def place(owner, h):
        return pl.ds(pl.multiple_of(owner * width + h * HD, HD), HD)

    def rows_of(owner):
        return pl.ds(pl.multiple_of(owner * own_rows, CH), own_rows)

    def hand_over(h, k):
        to = lax.rem(mine + k, groups)
        return pltpu.make_async_remote_copy(
            src_ref=finished.at[h, rows_of(to), :],
            dst_ref=exchanged.at[:, place(mine, h)],
            send_sem=row_send.at[h, to],
            recv_sem=row_recv.at[h, mine],
            device_id={"head": to},
            device_id_type=MESH,
        )

    def take_over(h, k):
        source = lax.rem(mine + k, groups)
        return pltpu.make_async_remote_copy(
            src_ref=finished.at[h, rows_of(source), :],
            dst_ref=exchanged.at[:, place(source, h)],
            send_sem=row_send.at[h, source],
            recv_sem=row_recv.at[h, source],
            device_id={"head": source},
            device_id_type=MESH,
        )

    t = lax.broadcasted_iota(jnp.int32, (CH, CH), 0)
    s = lax.broadcasted_iota(jnp.int32, (CH, CH), 1)
    causal = t >= s
    twin = mine + 1 - 2 * lax.rem(mine, 2)
    depth = w_ref.shape[0]
    piece = depth // PARTS

    def weights(owner, part):
        return pl.ds(pl.multiple_of(owner * depth + part * piece, piece), piece)

    def share(k, part):
        to = twin if k == 0 else lax.rem(mine + 2 * k, groups)
        return pltpu.make_async_remote_copy(
            src_ref=w_ref.at[part * piece : (part + 1) * piece, :],
            dst_ref=gathered.at[weights(mine, part), :],
            send_sem=near_send.at[k, part],
            recv_sem=near_recv.at[k, part],
            device_id={"head": to},
            device_id_type=MESH,
        )

    def relay(k, part):
        source = lax.rem(mine + groups - 2 * k, groups)
        return pltpu.make_async_remote_copy(
            src_ref=gathered.at[weights(source, part), :],
            dst_ref=gathered.at[weights(source, part), :],
            send_sem=pass_send.at[k, part],
            recv_sem=pass_recv.at[k, part],
            device_id={"head": twin},
            device_id_type=MESH,
        )

    keep = pltpu.make_async_copy(w_ref, gathered.at[weights_of(mine, depth), :], own_sem)
    keep.start()
    for part in range(PARTS):
        for k in range(1, groups // 2):
            share(k, part).start()
    for part in range(PARTS):
        share(0, part).start()

    for h in range(local_heads):

        def pass_on(m, carry):
            c = h * M + m

            @pl.when(me > 0)
            def _():
                copy(c).wait_recv()

            arrived = inbox[c].astype(jnp.float32)
            current[m] = arrived

            @pl.when(me < size - 1)
            def _():
                outbox[c] = (prod_ref[c] * arrived + mem_ref[c]).astype(jnp.bfloat16)
                copy(c).start()

            return carry

        lax.fori_loop(0, M, pass_on, 0)
        cols = slice(h * HD, (h + 1) * HD)

        def block(b, carry):
            rows = pl.ds(pl.multiple_of(b * CH, CH), CH)
            at = (b * local_heads + h) * 2
            entering = (
                state_ref[b * local_heads + h].astype(jnp.float32)
                + entry_ref[at] * current[chosen[at]]
                + entry_ref[at + 1] * current[chosen[at + 1]]
            ).astype(jnp.bfloat16)
            query, keys, values = q_ref[rows, cols], key_ref[rows, cols], v_ref[rows, cols]
            column = column_ref[rows, h : h + 1]
            line = line_ref[b, h : h + 1, :]
            gaps = jnp.where(causal, column - line, 0.0)
            decays = jnp.where(causal, jnp.exp(gaps), 0.0)
            scores = lax.dot_general(
                query, keys, (((1,), (1,)), ((), ())), preferred_element_type=jnp.float32
            )
            weighted = (scores * decays).astype(jnp.bfloat16)
            within = jnp.dot(weighted, values, preferred_element_type=jnp.float32)
            carried = jnp.dot(query, entering, preferred_element_type=jnp.float32)
            total = jnp.exp(column) * carried + (shares[at] + shares[at + 1]) * within
            scale = lax.rsqrt(jnp.mean(total * total, axis=-1, keepdims=True) + 1e-06)
            finished[h, rows, :] = (total * scale * gain_ref[:, cols]).astype(jnp.bfloat16)
            return carry

        lax.fori_loop(0, blocks, block, 0, unroll=4)
        for k in range(1, groups):
            hand_over(h, k).start()
        exchanged[:, place(mine, h)] = finished[h, rows_of(mine), :]

    for part in range(PARTS):
        for k in range(1, groups // 2):
            share(k, part).wait_recv()
            relay(k, part).start()

    for h in range(local_heads):
        for k in range(1, groups):
            take_over(h, k).wait_recv()

    keep.wait()
    for part in range(PARTS):
        share(0, part).wait_recv()
        for k in range(1, groups // 2):
            relay(k, part).wait_recv()
            relay(k, part).wait_send()
        for k in range(groups // 2):
            share(k, part).wait_send()

    @pl.when(me < size - 1)
    def _():
        def drain(c, carry):
            copy(c).wait_send()
            return carry

        lax.fori_loop(0, pieces, drain, 0)

    for h in range(local_heads):
        for k in range(1, groups):
            hand_over(h, k).wait_send()


def per_device(
    tokens, w_query, w_key, w_value, w_out, norm_gain, forget_rate, routing, memory_blend_share
):
    tok_rows = tokens.shape[0]
    width = w_query.shape[1]
    local_heads = width // HD
    num_blocks = tok_rows // CH
    groups = lax.axis_size("head")
    own_rows = tok_rows // groups
    pieces = local_heads * M

    def project(weight):
        return jnp.dot(tokens, weight, preferred_element_type=jnp.float32).astype(jnp.bfloat16)

    key_raw, value_rows, query = project(w_key), project(w_value), project(w_query)
    chosen, shares = routing.reshape(-1), memory_blend_share.reshape(-1)
    smem = pl.BlockSpec(memory_space=SMEM)
    vmem = pl.BlockSpec(memory_space=VMEM)
    keys, states, memory, columns, lines, entry, products = pl.pallas_call(
        local_kernel,
        out_shape=(
            jax.ShapeDtypeStruct((tok_rows, width), jnp.bfloat16),
            jax.ShapeDtypeStruct((num_blocks * local_heads, HD, HD), jnp.bfloat16),
            jax.ShapeDtypeStruct((pieces, HD, HD), jnp.float32),
            jax.ShapeDtypeStruct((tok_rows, local_heads), jnp.float32),
            jax.ShapeDtypeStruct((num_blocks, local_heads, CH), jnp.float32),
            jax.ShapeDtypeStruct((num_blocks * local_heads * 2, 1, HD), jnp.float32),
            jax.ShapeDtypeStruct((pieces, 1, HD), jnp.float32),
        ),
        in_specs=[smem] * 2 + [vmem] * 3,
        out_specs=(vmem,) * 7,
        compiler_params=pltpu.CompilerParams(vmem_limit_bytes=LIMIT),
        name="local",
    )(chosen, shares, key_raw, value_rows, forget_rate)
    exchanged, whole_out = pl.pallas_call(
        chain_kernel,
        out_shape=(
            jax.ShapeDtypeStruct((own_rows, groups * width), jnp.bfloat16),
            jax.ShapeDtypeStruct((groups * w_out.shape[0], w_out.shape[1]), jnp.bfloat16),
        ),
        in_specs=[smem] * 2 + [vmem] * 11,
        out_specs=(vmem, pl.BlockSpec(memory_space=pltpu.HBM)),
        scratch_shapes=[
            VMEM((pieces, HD, HD), jnp.bfloat16),
            VMEM((pieces, HD, HD), jnp.bfloat16),
            VMEM((M, HD, HD), jnp.float32),
            VMEM((local_heads, tok_rows, HD), jnp.bfloat16),
            pltpu.SemaphoreType.DMA((pieces,)),
            pltpu.SemaphoreType.DMA((pieces,)),
            pltpu.SemaphoreType.DMA((local_heads, groups)),
            pltpu.SemaphoreType.DMA((local_heads, groups)),
            pltpu.SemaphoreType.DMA,
            pltpu.SemaphoreType.DMA((groups // 2, PARTS)),
            pltpu.SemaphoreType.DMA((groups // 2, PARTS)),
            pltpu.SemaphoreType.DMA((groups // 2, PARTS)),
            pltpu.SemaphoreType.DMA((groups // 2, PARTS)),
        ],
        compiler_params=pltpu.CompilerParams(
            collective_id=0, has_side_effects=True, vmem_limit_bytes=LIMIT
        ),
        name="chain",
    )(
        chosen,
        shares,
        entry,
        products,
        memory,
        query,
        keys,
        value_rows,
        columns,
        lines,
        states,
        norm_gain[None],
        w_out,
    )
    result = jnp.dot(exchanged, whole_out, preferred_element_type=jnp.float32)
    return result.astype(jnp.bfloat16)


def solution(mesh):
    placed = (
        P("seq", None),
        P(None, "head"),
        P(None, "head"),
        P(None, "head"),
        P("head", None),
        P("head"),
        P("seq", "head"),
        P("seq", "head", None),
        P("seq", "head", None),
    )
    return jax.shard_map(
        per_device, mesh=mesh, in_specs=placed, out_specs=P(("seq", "head"), None), check_vma=False
    )
```
